512 devices in a mesh: dom: 128 (over z, y, core), sub: 4 (over x).
Axes of the slice: x: 4, y: 8, z: 8, core: 2. Of those that a mesh axis runs over, the one named last changes fastest.
Arguments:
- positions: float32 [3, 1048576], P(None, ('dom', 'sub')), may hold values from -6 to 6
- fixed_mask: int32 [1048576], P(('dom', 'sub')), may hold values 0 or 1
- send_count: int32 [128, 4, 5, 4], P('dom', 'sub'), may hold values from 0 to 128, as said below
- send_list: int32 [128, 4, 5, 4, 128], P('dom', 'sub'), may hold values from 0 to 2047, as said below
- block_nodes: int32 [64, 65536], P(None, ('dom', 'sub')), may hold values from 0 to 4607, as said below
- tet_corners: int32 [4, 8388608], P(None, ('dom', 'sub')), may hold values from 0 to 63, as said below
Outputs:
- smoothed: float32 [3, 1048576], P(None, ('dom', 'sub'))
The draws below stay inside these ranges and needn't reach their ends.
Inputs may be any that keep to these rules, and one draw needn't show every extreme that they name: send_count[d, s, k, t] is the number of nodes that partition (d, s) sends to the partition at dom index (d + k - 2) modulo the dom axis's size and sub index t; it is zero for k = 2, t = s. send_list[d, s, k, t, j] for j below send_count[d, s, k, t] is the local index of an owned node of partition (d, s), sent to that neighbour's ghost slot (k, s, j); later entries are ignored. `block_nodes`: entries are local columns of the block's partition: below 2048 an owned node, else 2048 + (k * 4 + t) * 128 + j for a ghost slot whose j is below the sending partition's count. `tet_corners`: the four corners of a tetrahedron are distinct rows.
All inputs are finite; a program needn't handle non-finite values. No bound on the sum of `fixed_mask` on one device may be relied on, other than what follows from the above.
Results may differ from the reference program's by a relative error of at most 0.0003.
Values sent between devices are 32-bit elements; how exact they have to be, the bound alone decides.
A program may use at most 128 MiB of HBM per device.

```python
import math
import jax
import jax.numpy as jnp
from jax import lax

NBLK = 128
NOWN = 2048
GSLOT = 128
REACH = 2
ITERS = 2
NODES = 1048576
N_DOM = 128
N_SUB = 4


def ghost_counts(key):
    slot_count = 2 * REACH + 1
    counts = jax.random.randint(jax.random.fold_in(key, 11), (N_DOM, N_SUB, slot_count, N_SUB), GSLOT // 8, GSLOT + 1)
    k = jnp.arange(slot_count)[None, None, :, None]
    s = jnp.arange(N_SUB)[None, :, None, None]
    t = jnp.arange(N_SUB)[None, None, None, :]
    counts = jnp.where((k == slot_count - 1) & (t == N_SUB - 1), GSLOT, counts)
    counts = jnp.where((k == REACH) & (t == s), 0, counts)
    return counts.astype(jnp.int32)


def draw_send_count(key, part):
    return ghost_counts(key)


def draw_send_list(key, part):
    slot_count = 2 * REACH + 1
    lists = jax.random.randint(jax.random.fold_in(key, 12), (N_DOM, N_SUB, slot_count, N_SUB, GSLOT), 0, NOWN)
    lists = lists.at[:, :, 0, 0, 0].set(0)
    lists = lists.at[:, :, 0, 0, 1].set(NOWN - 1)
    return lists.astype(jnp.int32)


def draw_block_nodes(key, part):
    counts = ghost_counts(key)
    slot_count = 2 * REACH + 1
    block_total = NBLK * N_DOM * N_SUB
    grid = (64, block_total)
    part_id = jnp.arange(block_total) // NBLK
    d = (part_id // N_SUB)[None, :]
    s = (part_id % N_SUB)[None, :]
    is_ghost = jax.random.randint(jax.random.fold_in(key, 21), grid, 0, 3) == 0
    k = jax.random.randint(jax.random.fold_in(key, 22), grid, 0, slot_count)
    t = jax.random.randint(jax.random.fold_in(key, 23), grid, 0, N_SUB)
    src_dom = (d - k + REACH) % N_DOM
    live = counts[src_dom, t, k, jnp.broadcast_to(s, grid)]
    j = jax.random.randint(jax.random.fold_in(key, 24), grid, 0, 1 << 20) % jnp.maximum(live, 1)
    ghost_col = NOWN + (k * N_SUB + t) * GSLOT + j
    owned_col = jax.random.randint(jax.random.fold_in(key, 25), grid, 0, NOWN)
    columns = jnp.where(is_ghost & (live > 0), ghost_col, owned_col)
    top_col = NOWN + slot_count * N_SUB * GSLOT - 1
    first_block = jnp.arange(block_total) % NBLK == 0
    forced = first_block & (part_id % N_SUB == N_SUB - 1)
    columns = columns.at[0].set(jnp.where(forced, top_col, columns[0]))
    columns = columns.at[1].set(jnp.where(first_block, 0, columns[1]))
    return columns.astype(jnp.int32)


def draw_tet_corners(key, part):
    tet_total = NBLK * 128 * N_DOM * N_SUB
    base = jax.random.randint(jax.random.fold_in(key, 31), (1, tet_total), 0, 64)
    jitter = jax.random.randint(jax.random.fold_in(key, 32), (4, tet_total), 0, 16)
    lanes = jnp.arange(4)[:, None] * 16
    corners = (base + lanes + jitter) % 64
    corners = corners.at[:, 0].set(jnp.array([0, 21, 42, 63]))
    return corners.astype(jnp.int32)


def touch_ends(entries, stream_key, low, largest):
    longest = entries.shape.index(max(entries.shape))
    spots = []
    for shift in (0, 1):
        where = [jax.random.randint(jax.random.fold_in(stream_key, axis), (), 0, length) for axis, length in enumerate(entries.shape)]
        where[longest] = (where[longest] + shift) % entries.shape[longest]
        spots.append(tuple(where))
    return entries.at[spots[0]].set(low).at[spots[1]].set(largest)


def level_of(rng, extent, split, least, top_value):
    factor_of = 1.0
    for axis_at, shards_of in split:
        draws = jax.random.uniform(jax.random.fold_in(jax.random.fold_in(rng, 6), axis_at), (shards_of,), jnp.float32, least / len(split), top_value / len(split))
        factor_of = factor_of * jnp.repeat(jnp.exp(draws), extent[axis_at] // shards_of).reshape((-1,) + (1,) * (len(extent) - 1 - axis_at))
    return factor_of


def scatter_about(stream_key, extent, deviation, reach, cuts=(), kind=jnp.bfloat16):
    entries = jax.random.normal(stream_key, extent, jnp.float32) * deviation
    if len(cuts) > 0:
        entries = level_of(stream_key, extent, cuts, -0.22, 0.18) * entries
    return jnp.clip(entries, min=-reach, max=reach).astype(kind)


def setup_inputs(seed: int = 0) -> dict:
    seeds = jax.random.split(jax.random.key(seed), 7)
    positions = scatter_about(seeds[0], (3, NODES), 1.0, 6.0, ((1, 512),), jnp.float32)
    fixed_mask = touch_ends((jax.random.randint(seeds[1], (NODES,), 0, 8) < 1).astype(jnp.int32), jax.random.fold_in(seeds[1], 1), 0, 1)
    send_count = draw_send_count(jax.random.fold_in(seeds[6], 71), 0)
    send_list = draw_send_list(jax.random.fold_in(seeds[6], 71), 0)
    block_nodes = draw_block_nodes(jax.random.fold_in(seeds[6], 71), 0)
    tet_corners = draw_tet_corners(jax.random.fold_in(seeds[6], 71), 0)
    return {"positions": positions, "fixed_mask": fixed_mask, "send_count": send_count, "send_list": send_list, "block_nodes": block_nodes, "tet_corners": tet_corners}


delta_reg = 2.0
step_size = 0.01
winv_rows = ((1.0, -1.0 / math.sqrt(3.0), -1.0 / math.sqrt(6.0)), (0.0, 2.0 / math.sqrt(3.0), -1.0 / math.sqrt(6.0)), (0.0, 0.0, math.sqrt(1.5)))

def tet_energy(local_nodes, block_nodes, tet_corners):
    block_total = block_nodes.shape[1]
    tet_total = tet_corners.shape[1]
    owner_block = jnp.arange(tet_total, dtype=jnp.int32) // 128
    flat_nodes = block_nodes.reshape(-1)
    node_ids = flat_nodes[tet_corners * block_total + owner_block[None, :]]
    corners = local_nodes[:, node_ids]
    edge_rows = [[corners[r, m + 1] - corners[r, 0] for m in range(3)] for r in range(3)]
    shape_mat = []
    for r in range(3):
        row_vals = []
        for c in range(3):
            acc_val = None
            for m in range(3):
                if winv_rows[m][c] != 0.0:
                    term_val = edge_rows[r][m] * winv_rows[m][c]
                    acc_val = term_val if acc_val is None else acc_val + term_val
            row_vals.append(acc_val)
        shape_mat.append(row_vals)
    norm_sq = shape_mat[0][0] * shape_mat[0][0]
    for r in range(3):
        for c in range(3):
            if r + c > 0:
                norm_sq = norm_sq + shape_mat[r][c] * shape_mat[r][c]
    volume_det = shape_mat[0][0] * (shape_mat[1][1] * shape_mat[2][2] - shape_mat[1][2] * shape_mat[2][1]) - shape_mat[0][1] * (shape_mat[1][0] * shape_mat[2][2] - shape_mat[1][2] * shape_mat[2][0]) + shape_mat[0][2] * (shape_mat[1][0] * shape_mat[2][1] - shape_mat[1][1] * shape_mat[2][0])
    root_term = jnp.sqrt(volume_det * volume_det + 4.0 * delta_reg * delta_reg)
    upper_part = 0.5 * (volume_det + root_term)
    lower_den = jnp.where(volume_det < 0, root_term - volume_det, 1.0)
    height = jnp.where(volume_det >= 0, upper_part, 2.0 * delta_reg * delta_reg / lower_den)
    distortion = norm_sq / (3.0 * height ** (2.0 / 3.0))
    return jnp.sum(distortion)

def reference(positions, fixed_mask, send_count, send_list, block_nodes, tet_corners):
    dom_count = N_DOM
    sub_count = N_SUB
    slot_count = 2 * REACH + 1
    part_count = dom_count * sub_count
    d = jnp.arange(dom_count, dtype=jnp.int32)[:, None, None, None, None]
    s = jnp.arange(sub_count, dtype=jnp.int32)[None, :, None, None, None]
    k = jnp.arange(slot_count, dtype=jnp.int32)[None, None, :, None, None]
    t = jnp.arange(sub_count, dtype=jnp.int32)[None, None, None, :, None]
    j = jnp.arange(GSLOT, dtype=jnp.int32)[None, None, None, None, :]
    src_dom = (d - k + REACH) % dom_count
    entry_ids = send_list[src_dom, t, k, s, j]
    live_count = send_count[src_dom, t, k, s]
    ghost_ok = (j < live_count).reshape(part_count, -1)
    ghost_ids = ((src_dom * sub_count + t) * NOWN + entry_ids).astype(jnp.int32).reshape(part_count, -1)
    blocks_all = block_nodes.reshape(64, part_count, NBLK).transpose(1, 0, 2)
    corners_all = tet_corners.reshape(4, part_count, NBLK * 128).transpose(1, 0, 2)
    free_nodes = (fixed_mask == 0).astype(positions.dtype)
    grad_fn = jax.grad(tet_energy)
    current = positions
    for step in range(ITERS):

        def visit_part(grad_total, item):
            part, ids_here, ok_here, blocks, corners = item
            start = part * NOWN
            owned_pos = lax.dynamic_slice_in_dim(current, start, NOWN, 1)
            ghosts = jnp.where(ok_here[None, :], current[:, ids_here], 0.0)
            local_nodes = jnp.concatenate([owned_pos, ghosts], axis=1)
            local_grad = grad_fn(local_nodes, blocks, corners)
            own_part = lax.dynamic_slice_in_dim(grad_total, start, NOWN, 1) + local_grad[:, :NOWN]
            grad_total = lax.dynamic_update_slice_in_dim(grad_total, own_part, start, 1)
            grad_total = grad_total.at[:, ids_here].add(jnp.where(ok_here[None, :], local_grad[:, NOWN:], 0.0))
            return (grad_total, None)
        grad_total, _ = lax.scan(visit_part, jnp.zeros_like(current), (jnp.arange(part_count, dtype=jnp.int32), ghost_ids, ghost_ok, blocks_all, corners_all))
        current = current - step_size * free_nodes[None, :] * grad_total
    return current
```

```python
import functools
import math

import jax
import jax.numpy as jnp
from jax import lax
from jax.experimental import pallas as pl
from jax.experimental.pallas import tpu as pltpu
from jax.sharding import PartitionSpec as P

ITERS = 2
STEP = 0.01
DELTA = 2.0
REACH = 2
SLOTS = 5
SUBS = 4
NPAIR = SLOTS * SUBS
OWN_ROWS = 16
ROWS = OWN_ROWS + NPAIR
HPAD = 40
MESH = pl.DeviceIdType.MESH


def nt_dot(a, b):
    return lax.dot_general(a, b, (((1,), (1,)), ((), ())), preferred_element_type=jnp.float32)


def split_rows(x):
    low = x - x.astype(jnp.bfloat16).astype(jnp.float32)
    return jnp.concatenate([x, low], axis=0).astype(jnp.bfloat16)


def lane_take(row, lanes):
    src = jnp.broadcast_to(row, lanes.shape)
    return jnp.take_along_axis(src, lanes, axis=1, mode="promise_in_bounds")


def send_columns(list_ref, count_ref, cols_ref):
    lane = lax.broadcasted_iota(jnp.int32, (1, 128), 1)
    for k in range(SLOTS):
        for t in range(SUBS):
            row = list_ref[0, 0, k, t : t + 1, :]
            cols_ref[k * SUBS + t : k * SUBS + t + 1, :] = jnp.where(lane < count_ref[0, 0, k, t], row, -1)


def gather_payload(pos_ref, cols_ref, pay_ref):
    cols = jnp.concatenate([cols_ref[...], jnp.full((24 - NPAIR, 128), -1, jnp.int32)], axis=0)
    high = cols >> 7
    low = cols & 127
    for r in range(3):
        acc = jnp.zeros((24, 128), jnp.float32)
        for h in range(OWN_ROWS):
            picked = lane_take(pos_ref[r * OWN_ROWS + h : r * OWN_ROWS + h + 1, :], low)
            acc = jnp.where(high == h, picked, acc)
        for n in range(NPAIR):
            pay_ref[n, r : r + 1, :] = acc[n : n + 1, :]
    for n in range(NPAIR):
        pay_ref[n, 3:4, :] = jnp.zeros((1, 128), jnp.float32)


def tet_gradient(corner):
    edge = [[corner[m + 1][r] - corner[0][r] for r in range(3)] for m in range(3)]
    total = [edge[0][r] + edge[1][r] + edge[2][r] for r in range(3)]
    squares = None
    for m in range(3):
        for r in range(3):
            term = edge[m][r] * edge[m][r]
            squares = term if squares is None else squares + term
    spread = total[0] * total[0] + total[1] * total[1] + total[2] * total[2]
    norm_sq = 2.0 * squares - 0.5 * spread

    def cross(a, b):
        return [
            a[1] * b[2] - a[2] * b[1],
            a[2] * b[0] - a[0] * b[2],
            a[0] * b[1] - a[1] * b[0],
        ]

    cof = [cross(edge[1], edge[2]), cross(edge[2], edge[0]), cross(edge[0], edge[1])]
    root2 = math.sqrt(2.0)
    det = root2 * (edge[0][0] * cof[0][0] + edge[0][1] * cof[0][1] + edge[0][2] * cof[0][2])
    root = jnp.sqrt(det * det + 4.0 * DELTA * DELTA)
    far = root + jnp.abs(det)
    height = jnp.where(det >= 0, 0.5 * far, (2.0 * DELTA * DELTA) / far)
    factor = (2.0 / 3.0) * jnp.exp((-2.0 / 3.0) * jnp.log(height))
    pull = (root2 / 3.0) * norm_sq / root
    grads = []
    for m in range(3):
        grads.append([factor * (2.0 * edge[m][r] - 0.5 * total[r] - pull * cof[m][r]) for r in range(3)])
    first = [-(grads[0][r] + grads[1][r] + grads[2][r]) for r in range(3)]
    return [first] + grads


def prepare_blocks(nodes_ref, packed_ref):
    turned = nodes_ref[...].T
    packed_ref[...] = jnp.concatenate([turned[0:64, :], turned[64:128, :]], axis=1)


def local_gradient(pos_ref, ghost_ref, packed_ref, corners_ref, spread_ref, acc_ref):
    acc_ref[...] = jnp.zeros_like(acc_ref)

    def body(j, carry):
        base = pl.multiple_of(j * 8, 8)
        cols = packed_ref[pl.ds(base, 8), :]
        high = cols >> 7
        low = cols & 127
        source = []
        for r in range(3):
            picked = jnp.zeros((8, 128), jnp.float32)
            for h in range(ROWS):
                if h < OWN_ROWS:
                    row = pos_ref[r * OWN_ROWS + h : r * OWN_ROWS + h + 1, :]
                else:
                    row = ghost_ref[h - OWN_ROWS, r : r + 1, :]
                picked = jnp.where(high == h, lane_take(row, low), picked)
            source.append(picked)
        for half in range(2):
            block = half * 64 + base
            corner = []
            for c in range(4):
                lanes = corners_ref[pl.ds(block * 4 + c, 8, stride=4), :] + 64 * half
                corner.append([jnp.take_along_axis(source[r], lanes, axis=1, mode="promise_in_bounds") for r in range(3)])
            grads = tet_gradient(corner)
            for c in range(4):
                for r in range(3):
                    start = (c * 3 + r) * 16 + half * 8
                    spread_ref[start : start + 8, :] = grads[c][r]
        node_iota = lax.broadcasted_iota(jnp.int32, (64, 128), 0)
        high_iota = lax.broadcasted_iota(jnp.int32, (HPAD, 128), 0)
        low_iota = lax.broadcasted_iota(jnp.int32, (128, 128), 0)
        left_parts = []
        right_parts = []
        for i in range(8):
            sums = []
            for half in range(2):
                parts = []
                marks = []
                for c in range(4):
                    rows = spread_ref[pl.ds(c * 48 + half * 8 + i, 8, stride=16), :]
                    parts.append(split_rows(rows))
                    ids = corners_ref[pl.ds((half * 64 + base + i) * 4 + c, 1), :]
                    marks.append(jnp.where(node_iota == ids, 1.0, 0.0).astype(jnp.bfloat16))
                out = nt_dot(jnp.concatenate(parts, axis=1), jnp.concatenate(marks, axis=1))
                sums.append(out[0:8, :] + out[8:16, :])
            pair = jnp.concatenate(sums, axis=1)
            pair_low = pair - pair.astype(jnp.bfloat16).astype(jnp.float32)
            chosen = high_iota == high[i : i + 1, :]
            stack = [jnp.where(chosen, pair[r : r + 1, :], 0.0) for r in range(3)]
            stack += [jnp.where(chosen, pair_low[r : r + 1, :], 0.0) for r in range(3)]
            left_parts.append(jnp.concatenate(stack, axis=0).astype(jnp.bfloat16))
            right_parts.append(jnp.where(low_iota == low[i : i + 1, :], 1.0, 0.0).astype(jnp.bfloat16))
        acc_ref[...] += nt_dot(jnp.concatenate(left_parts, axis=1), jnp.concatenate(right_parts, axis=1))
        return carry

    lax.fori_loop(0, 8, body, 0)


def put_gradient(acc_ref, own_ref, out_ref):
    for r in range(3):
        both = acc_ref[r * HPAD : (r + 1) * HPAD, :] + acc_ref[(3 + r) * HPAD : (4 + r) * HPAD, :]
        own_ref[r * OWN_ROWS : (r + 1) * OWN_ROWS, :] = both[0:OWN_ROWS, :]
        for n in range(NPAIR):
            out_ref[n, r : r + 1, :] = both[OWN_ROWS + n : OWN_ROWS + n + 1, :]
    for n in range(NPAIR):
        out_ref[n, 3:4, :] = jnp.zeros((1, 128), jnp.float32)


def returned_gradient(back_ref, cols_ref):
    high_iota = lax.broadcasted_iota(jnp.int32, (OWN_ROWS, 128), 0)
    low_iota = lax.broadcasted_iota(jnp.int32, (128, 128), 0)
    left_parts = []
    right_parts = []
    for n in range(NPAIR):
        cols = cols_ref[n : n + 1, :]
        chosen = high_iota == (cols >> 7)
        values = jnp.where(cols >= 0, back_ref[n], 0.0)
        lows = values - values.astype(jnp.bfloat16).astype(jnp.float32)
        stack = [jnp.where(chosen, values[r : r + 1, :], 0.0) for r in range(3)]
        stack += [jnp.where(chosen, lows[r : r + 1, :], 0.0) for r in range(3)]
        left_parts.append(jnp.concatenate(stack, axis=0).astype(jnp.bfloat16))
        right_parts.append(jnp.where(low_iota == (cols & 127), 1.0, 0.0).astype(jnp.bfloat16))
    out = nt_dot(jnp.concatenate(left_parts, axis=1), jnp.concatenate(right_parts, axis=1))
    return out[0:48, :] + out[48:96, :]


def moved(pos_ref, mask_ref, own_ref, back_ref, cols_ref):
    grad = own_ref[...] + returned_gradient(back_ref, cols_ref)
    free = jnp.where(mask_ref[...] == 0, STEP, 0.0)
    return pos_ref[...] - jnp.concatenate([free, free, free], axis=0) * grad


def load_positions(raw_ref, pos_ref):
    for r in range(3):
        for h in range(OWN_ROWS):
            pos_ref[r * OWN_ROWS + h : r * OWN_ROWS + h + 1, :] = raw_ref[r : r + 1, h * 128 : (h + 1) * 128]


def store_positions(value, raw_ref):
    for r in range(3):
        for h in range(OWN_ROWS):
            raw_ref[r : r + 1, h * 128 : (h + 1) * 128] = value[r * OWN_ROWS + h : r * OWN_ROWS + h + 1, :]


def start_kernel(raw_ref, list_ref, count_ref, nodes_ref, pos_ref, cols_ref, packed_ref, pay_ref):
    load_positions(raw_ref, pos_ref)
    send_columns(list_ref, count_ref, cols_ref)
    prepare_blocks(nodes_ref, packed_ref)
    gather_payload(pos_ref, cols_ref, pay_ref)


def gradient_kernel(pos_ref, ghost_ref, packed_ref, corners_ref, own_ref, out_ref, spread_ref, acc_ref):
    spread_ref[192:320, :] = jnp.zeros((128, 128), jnp.float32)
    local_gradient(pos_ref, ghost_ref, packed_ref, corners_ref, spread_ref, acc_ref)
    put_gradient(acc_ref, own_ref, out_ref)


def step_kernel(pos_ref, mask_ref, own_ref, back_ref, cols_ref, next_ref, pay_ref):
    next_ref[...] = moved(pos_ref, mask_ref, own_ref, back_ref, cols_ref)
    gather_payload(next_ref, cols_ref, pay_ref)


def last_kernel(pos_ref, mask_ref, own_ref, back_ref, cols_ref, raw_ref):
    store_positions(moved(pos_ref, mask_ref, own_ref, back_ref, cols_ref), raw_ref)


def partners(sign):
    dom = lax.axis_index("dom")
    sub = lax.axis_index("sub")
    doms = lax.axis_size("dom")
    found = []
    for k in range(SLOTS):
        for turn in range(SUBS):
            if k == REACH and turn == 0:
                continue
            there = lax.rem(dom + sign * (k - REACH) + doms, doms)
            found.append((k, turn, there, lax.rem(sub + turn, SUBS)))
    return found


def exchange_kernel(sign, src_ref, dst_ref, send_sem, recv_sem):
    sub = lax.axis_index("sub")
    found = partners(sign)
    barrier = pltpu.get_barrier_semaphore()
    for k, turn, there, t in found:
        pl.semaphore_signal(barrier, inc=1, device_id=(there, t), device_id_type=MESH)
    pl.semaphore_wait(barrier, len(found))
    copies = []
    for k, turn, there, t in found:
        copies.append(
            pltpu.make_async_remote_copy(
                src_ref=src_ref.at[k * SUBS + t],
                dst_ref=dst_ref.at[k * SUBS + sub],
                send_sem=send_sem.at[k * SUBS + turn],
                recv_sem=recv_sem.at[k * SUBS + turn],
                device_id=(there, t),
                device_id_type=MESH,
            )
        )
    for copy in copies:
        copy.start()
    dst_ref[REACH * SUBS + sub] = src_ref[REACH * SUBS + sub]
    for copy in copies:
        copy.wait()


VMEM = pl.BlockSpec(memory_space=pltpu.VMEM)
SMEM = pl.BlockSpec(memory_space=pltpu.SMEM)


def shape(*dims, dtype=jnp.float32):
    return jax.ShapeDtypeStruct(dims, dtype)


def exchange(value, sign):
    return pl.pallas_call(
        functools.partial(exchange_kernel, sign),
        out_shape=shape(NPAIR, 4, 128),
        in_specs=[VMEM],
        out_specs=VMEM,
        scratch_shapes=[pltpu.SemaphoreType.DMA((NPAIR,)), pltpu.SemaphoreType.DMA((NPAIR,))],
        compiler_params=pltpu.CompilerParams(collective_id=0 if sign > 0 else 1, has_side_effects=True),
        name="forward" if sign > 0 else "back",
    )(value)


def gradient(pos, ghosts, packed, corners):
    return pl.pallas_call(
        gradient_kernel,
        out_shape=(shape(48, 128), shape(NPAIR, 4, 128)),
        in_specs=[VMEM] * 4,
        out_specs=(VMEM, VMEM),
        scratch_shapes=[pltpu.VMEM((320, 128), jnp.float32), pltpu.VMEM((6 * HPAD, 128), jnp.float32)],
        name="gradient",
    )(pos, ghosts, packed, corners)


def per_device(positions, fixed_mask, send_count, send_list, block_nodes, tet_corners):
    corners = tet_corners.reshape(4, 128, 128).transpose(1, 0, 2).reshape(512, 128)
    mask = fixed_mask.reshape(OWN_ROWS, 128)
    pos, cols, packed, pay = pl.pallas_call(
        start_kernel,
        out_shape=(
            shape(48, 128),
            shape(NPAIR, 128, dtype=jnp.int32),
            shape(64, 128, dtype=jnp.int32),
            shape(NPAIR, 4, 128),
        ),
        in_specs=[VMEM, VMEM, SMEM, VMEM],
        out_specs=(VMEM,) * 4,
        name="start",
    )(positions, send_list, send_count, block_nodes)
    for step in range(ITERS):
        ghosts = exchange(pay, 1)
        own, out = gradient(pos, ghosts, packed, corners)
        back = exchange(out, -1)
        if step < ITERS - 1:
            pos, pay = pl.pallas_call(
                step_kernel,
                out_shape=(shape(48, 128), shape(NPAIR, 4, 128)),
                in_specs=[VMEM] * 5,
                out_specs=(VMEM,) * 2,
                name="step",
            )(pos, mask, own, back, cols)
    return pl.pallas_call(
        last_kernel,
        out_shape=shape(3, 2048),
        in_specs=[VMEM] * 5,
        out_specs=VMEM,
        name="last",
    )(pos, mask, own, back, cols)


def solution(mesh):
    return jax.shard_map(
        per_device,
        mesh=mesh,
        in_specs=(
            P(None, ("dom", "sub")),
            P(("dom", "sub")),
            P("dom", "sub", None, None),
            P("dom", "sub", None, None, None),
            P(None, ("dom", "sub")),
            P(None, ("dom", "sub")),
        ),
        out_specs=P(None, ("dom", "sub")),
        check_vma=False,
    )
```

```python
import math

import jax
import jax.numpy as jnp
from jax import lax
from jax.experimental import pallas as pl
from jax.experimental.pallas import tpu as pltpu
from jax.sharding import PartitionSpec as P

ITERS = 2
STEP = 0.01
DELTA = 2.0
REACH = 2
SLOTS = 5
SUBS = 4
NPAIR = SLOTS * SUBS
OWN_ROWS = 16
ROWS = OWN_ROWS + NPAIR
HPAD = 40
MESH = pl.DeviceIdType.MESH


def nt_dot(a, b):
    return lax.dot_general(a, b, (((1,), (1,)), ((), ())), preferred_element_type=jnp.float32)


def split_rows(x):
    low = x - x.astype(jnp.bfloat16).astype(jnp.float32)
    return jnp.concatenate([x, low], axis=0).astype(jnp.bfloat16)


def lane_take(row, lanes):
    src = jnp.broadcast_to(row, lanes.shape)
    return jnp.take_along_axis(src, lanes, axis=1, mode="promise_in_bounds")


def send_columns(list_ref, count_ref, cols_ref):
    lane = lax.broadcasted_iota(jnp.int32, (1, 128), 1)
    for k in range(SLOTS):
        for t in range(SUBS):
            row = list_ref[0, 0, k, t : t + 1, :]
            cols_ref[k * SUBS + t : k * SUBS + t + 1, :] = jnp.where(lane < count_ref[0, 0, k, t], row, -1)


def gather_payload(pos_ref, cols_ref, pay_ref):
    cols = jnp.concatenate([cols_ref[...], jnp.full((24 - NPAIR, 128), -1, jnp.int32)], axis=0)
    high = cols >> 7
    low = cols & 127
    for r in range(3):
        acc = jnp.zeros((24, 128), jnp.float32)
        for h in range(OWN_ROWS):
            picked = lane_take(pos_ref[r * OWN_ROWS + h : r * OWN_ROWS + h + 1, :], low)
            acc = jnp.where(high == h, picked, acc)
        for n in range(NPAIR):
            pay_ref[n, r : r + 1, :] = acc[n : n + 1, :]
    for n in range(NPAIR):
        pay_ref[n, 3:4, :] = jnp.zeros((1, 128), jnp.float32)


def tet_gradient(corner):
    edge = [[corner[m + 1][r] - corner[0][r] for r in range(3)] for m in range(3)]
    total = [edge[0][r] + edge[1][r] + edge[2][r] for r in range(3)]
    squares = None
    for m in range(3):
        for r in range(3):
            term = edge[m][r] * edge[m][r]
            squares = term if squares is None else squares + term
    spread = total[0] * total[0] + total[1] * total[1] + total[2] * total[2]
    norm_sq = 2.0 * squares - 0.5 * spread

    def cross(a, b):
        return [
            a[1] * b[2] - a[2] * b[1],
            a[2] * b[0] - a[0] * b[2],
            a[0] * b[1] - a[1] * b[0],
        ]

    cof = [cross(edge[1], edge[2]), cross(edge[2], edge[0]), cross(edge[0], edge[1])]
    root2 = math.sqrt(2.0)
    det = root2 * (edge[0][0] * cof[0][0] + edge[0][1] * cof[0][1] + edge[0][2] * cof[0][2])
    root = jnp.sqrt(det * det + 4.0 * DELTA * DELTA)
    far = root + jnp.abs(det)
    height = jnp.where(det >= 0, 0.5 * far, (2.0 * DELTA * DELTA) / far)
    factor = (2.0 / 3.0) * jnp.exp((-2.0 / 3.0) * jnp.log(height))
    pull = (root2 / 3.0) * norm_sq / root
    grads = []
    for m in range(3):
        grads.append([factor * (2.0 * edge[m][r] - 0.5 * total[r] - pull * cof[m][r]) for r in range(3)])
    first = [-(grads[0][r] + grads[1][r] + grads[2][r]) for r in range(3)]
    return [first] + grads


def prepare_blocks(nodes_ref, packed_ref):
    turned = nodes_ref[...].T
    packed_ref[...] = jnp.concatenate([turned[0:64, :], turned[64:128, :]], axis=1)


def local_gradient(pos_ref, ghost_ref, packed_ref, corners_ref, spread_ref, acc_ref):
    acc_ref[...] = jnp.zeros_like(acc_ref)

    def body(j, carry):
        base = pl.multiple_of(j * 8, 8)
        cols = packed_ref[pl.ds(base, 8), :]
        high = cols >> 7
        low = cols & 127
        source = []
        for r in range(3):
            picked = jnp.zeros((8, 128), jnp.float32)
            for h in range(ROWS):
                if h < OWN_ROWS:
                    row = pos_ref[r * OWN_ROWS + h : r * OWN_ROWS + h + 1, :]
                else:
                    row = ghost_ref[h - OWN_ROWS, r : r + 1, :]
                picked = jnp.where(high == h, lane_take(row, low), picked)
            source.append(picked)
        for half in range(2):
            block = half * 64 + base
            corner = []
            for c in range(4):
                lanes = corners_ref[pl.ds(block * 4 + c, 8, stride=4), :] + 64 * half
                corner.append([jnp.take_along_axis(source[r], lanes, axis=1, mode="promise_in_bounds") for r in range(3)])
            grads = tet_gradient(corner)
            for c in range(4):
                for r in range(3):
                    start = (c * 3 + r) * 16 + half * 8
                    spread_ref[start : start + 8, :] = grads[c][r]
        node_iota = lax.broadcasted_iota(jnp.int32, (64, 128), 0)
        high_iota = lax.broadcasted_iota(jnp.int32, (HPAD, 128), 0)
        low_iota = lax.broadcasted_iota(jnp.int32, (128, 128), 0)
        left_parts = []
        right_parts = []
        for i in range(8):
            sums = []
            for half in range(2):
                parts = []
                marks = []
                for c in range(4):
                    rows = spread_ref[pl.ds(c * 48 + half * 8 + i, 8, stride=16), :]
                    parts.append(split_rows(rows))
                    ids = corners_ref[pl.ds((half * 64 + base + i) * 4 + c, 1), :]
                    marks.append(jnp.where(node_iota == ids, 1.0, 0.0).astype(jnp.bfloat16))
                out = nt_dot(jnp.concatenate(parts, axis=1), jnp.concatenate(marks, axis=1))
                sums.append(out[0:8, :] + out[8:16, :])
            pair = jnp.concatenate(sums, axis=1)
            pair_low = pair - pair.astype(jnp.bfloat16).astype(jnp.float32)
            chosen = high_iota == high[i : i + 1, :]
            stack = [jnp.where(chosen, pair[r : r + 1, :], 0.0) for r in range(3)]
            stack += [jnp.where(chosen, pair_low[r : r + 1, :], 0.0) for r in range(3)]
            left_parts.append(jnp.concatenate(stack, axis=0).astype(jnp.bfloat16))
            right_parts.append(jnp.where(low_iota == low[i : i + 1, :], 1.0, 0.0).astype(jnp.bfloat16))
        acc_ref[...] += nt_dot(jnp.concatenate(left_parts, axis=1), jnp.concatenate(right_parts, axis=1))
        return carry

    lax.fori_loop(0, 8, body, 0)


def put_gradient(acc_ref, own_ref, out_ref):
    for r in range(3):
        both = acc_ref[r * HPAD : (r + 1) * HPAD, :] + acc_ref[(3 + r) * HPAD : (4 + r) * HPAD, :]
        own_ref[r * OWN_ROWS : (r + 1) * OWN_ROWS, :] = both[0:OWN_ROWS, :]
        for n in range(NPAIR):
            out_ref[n, r : r + 1, :] = both[OWN_ROWS + n : OWN_ROWS + n + 1, :]
    for n in range(NPAIR):
        out_ref[n, 3:4, :] = jnp.zeros((1, 128), jnp.float32)


def returned_gradient(back_ref, cols_ref):
    high_iota = lax.broadcasted_iota(jnp.int32, (OWN_ROWS, 128), 0)
    low_iota = lax.broadcasted_iota(jnp.int32, (128, 128), 0)
    left_parts = []
    right_parts = []
    for n in range(NPAIR):
        cols = cols_ref[n : n + 1, :]
        chosen = high_iota == (cols >> 7)
        values = jnp.where(cols >= 0, back_ref[n], 0.0)
        lows = values - values.astype(jnp.bfloat16).astype(jnp.float32)
        stack = [jnp.where(chosen, values[r : r + 1, :], 0.0) for r in range(3)]
        stack += [jnp.where(chosen, lows[r : r + 1, :], 0.0) for r in range(3)]
        left_parts.append(jnp.concatenate(stack, axis=0).astype(jnp.bfloat16))
        right_parts.append(jnp.where(low_iota == (cols & 127), 1.0, 0.0).astype(jnp.bfloat16))
    out = nt_dot(jnp.concatenate(left_parts, axis=1), jnp.concatenate(right_parts, axis=1))
    return out[0:48, :] + out[48:96, :]


def moved(pos_ref, mask_ref, own_ref, back_ref, cols_ref):
    grad = own_ref[...] + returned_gradient(back_ref, cols_ref)
    free = jnp.where(mask_ref[...] == 0, STEP, 0.0)
    return pos_ref[...] - jnp.concatenate([free, free, free], axis=0) * grad


def load_positions(raw_ref, pos_ref):
    for r in range(3):
        for h in range(OWN_ROWS):
            pos_ref[r * OWN_ROWS + h : r * OWN_ROWS + h + 1, :] = raw_ref[r : r + 1, h * 128 : (h + 1) * 128]


def store_positions(value, raw_ref):
    for r in range(3):
        for h in range(OWN_ROWS):
            raw_ref[r : r + 1, h * 128 : (h + 1) * 128] = value[r * OWN_ROWS + h : r * OWN_ROWS + h + 1, :]


def partners(sign):
    dom = lax.axis_index("dom")
    sub = lax.axis_index("sub")
    doms = lax.axis_size("dom")
    found = []
    for k in range(SLOTS):
        for turn in range(SUBS):
            if k == REACH and turn == 0:
                continue
            there = lax.rem(dom + sign * (k - REACH) + doms, doms)
            found.append((k, turn, there, lax.rem(sub + turn, SUBS)))
    return found


def exchange(sign, found, src_ref, dst_ref, send_sem, recv_sem):
    sub = lax.axis_index("sub")
    copies = []
    for k, turn, there, t in found:
        copies.append(
            pltpu.make_async_remote_copy(
                src_ref=src_ref.at[k * SUBS + t],
                dst_ref=dst_ref.at[k * SUBS + sub],
                send_sem=send_sem.at[k * SUBS + turn],
                recv_sem=recv_sem.at[k * SUBS + turn],
                device_id=(there, t),
                device_id_type=MESH,
            )
        )
    for copy in copies:
        copy.start()
    dst_ref[REACH * SUBS + sub] = src_ref[REACH * SUBS + sub]
    for copy in copies:
        copy.wait()


def smooth_kernel(
    raw_ref,
    mask_ref,
    list_ref,
    count_ref,
    nodes_ref,
    corners_ref,
    done_ref,
    pos_ref,
    cols_ref,
    packed_ref,
    pay_ref,
    ghost_ref,
    out_ref,
    back_ref,
    own_ref,
    spread_ref,
    acc_ref,
    send_sem,
    recv_sem,
):
    ahead = partners(1)
    behind = partners(-1)
    barrier = pltpu.get_barrier_semaphore()
    for _, _, there, t in ahead:
        pl.semaphore_signal(barrier, inc=1, device_id=(there, t), device_id_type=MESH)
    load_positions(raw_ref, pos_ref)
    send_columns(list_ref, count_ref, cols_ref)
    prepare_blocks(nodes_ref, packed_ref)
    spread_ref[192:320, :] = jnp.zeros((128, 128), jnp.float32)
    gather_payload(pos_ref, cols_ref, pay_ref.at[0])
    pl.semaphore_wait(barrier, len(ahead))
    for step in range(ITERS):
        exchange(1, ahead, pay_ref.at[step], ghost_ref.at[step], send_sem.at[2 * step], recv_sem.at[2 * step])
        local_gradient(pos_ref, ghost_ref.at[step], packed_ref, corners_ref, spread_ref, acc_ref)
        put_gradient(acc_ref, own_ref, out_ref.at[step])
        exchange(-1, behind, out_ref.at[step], back_ref.at[step], send_sem.at[2 * step + 1], recv_sem.at[2 * step + 1])
        value = moved(pos_ref, mask_ref, own_ref, back_ref.at[step], cols_ref)
        if step < ITERS - 1:
            pos_ref[...] = value
            gather_payload(pos_ref, cols_ref, pay_ref.at[step + 1])
        else:
            store_positions(value, done_ref)


VMEM = pl.BlockSpec(memory_space=pltpu.VMEM)
SMEM = pl.BlockSpec(memory_space=pltpu.SMEM)


def per_device(positions, fixed_mask, send_count, send_list, block_nodes, tet_corners):
    corners = tet_corners.reshape(4, 128, 128).transpose(1, 0, 2).reshape(512, 128)
    mask = fixed_mask.reshape(OWN_ROWS, 128)
    slots = pltpu.VMEM((ITERS, NPAIR, 4, 128), jnp.float32)
    return pl.pallas_call(
        smooth_kernel,
        out_shape=jax.ShapeDtypeStruct((3, 2048), jnp.float32),
        in_specs=[VMEM, VMEM, VMEM, SMEM, VMEM, VMEM],
        out_specs=VMEM,
        scratch_shapes=[
            pltpu.VMEM((48, 128), jnp.float32),
            pltpu.VMEM((NPAIR, 128), jnp.int32),
            pltpu.VMEM((64, 128), jnp.int32),
            slots,
            slots,
            slots,
            slots,
            pltpu.VMEM((48, 128), jnp.float32),
            pltpu.VMEM((320, 128), jnp.float32),
            pltpu.VMEM((6 * HPAD, 128), jnp.float32),
            pltpu.SemaphoreType.DMA((2 * ITERS, NPAIR)),
            pltpu.SemaphoreType.DMA((2 * ITERS, NPAIR)),
        ],
        compiler_params=pltpu.CompilerParams(collective_id=0, has_side_effects=True),
        name="smooth",
    )(positions, mask, send_list, send_count, block_nodes, corners)


def solution(mesh):
    return jax.shard_map(
        per_device,
        mesh=mesh,
        in_specs=(
            P(None, ("dom", "sub")),
            P(("dom", "sub")),
            P("dom", "sub", None, None),
            P("dom", "sub", None, None, None),
            P(None, ("dom", "sub")),
            P(None, ("dom", "sub")),
        ),
        out_specs=P(None, ("dom", "sub")),
        check_vma=False,
    )
```

```python
import functools
import math

import jax
import jax.numpy as jnp
from jax import lax
from jax.experimental import pallas as pl
from jax.experimental.pallas import tpu as pltpu
from jax.sharding import PartitionSpec as P

ITERS = 2
STEP = 0.01
DELTA = 2.0
REACH = 2
SLOTS = 5
SUBS = 4
NPAIR = SLOTS * SUBS
OWN_ROWS = 16
ROWS = OWN_ROWS + NPAIR
GPAD = 24
GROUPS = 4
MESH = pl.DeviceIdType.MESH


def nt_dot(a, b):
    return lax.dot_general(a, b, (((1,), (1,)), ((), ())), preferred_element_type=jnp.float32)


def low_piece(x):
    return x - x.astype(jnp.bfloat16).astype(jnp.float32)


def lane_take(row, lanes):
    src = jnp.broadcast_to(row, lanes.shape)
    return jnp.take_along_axis(src, lanes, axis=1, mode="promise_in_bounds")


def send_columns(list_ref, count_ref, cols_ref):
    lane = lax.broadcasted_iota(jnp.int32, (1, 128), 1)
    for k in range(SLOTS):
        for t in range(SUBS):
            count = jnp.broadcast_to(count_ref[0, 0, t : t + 1, k : k + 1], (1, 128))
            row = list_ref[0, 0, k, t : t + 1, :]
            cols_ref[k * SUBS + t : k * SUBS + t + 1, :] = jnp.where(lane < count, row, -1)


def gather_payload(pos_ref, cols_ref, pay_ref):
    cols = jnp.concatenate([cols_ref[...], jnp.full((24 - NPAIR, 128), -1, jnp.int32)], axis=0)
    high = cols >> 7
    low = cols & 127
    for r in range(3):
        acc = jnp.zeros((24, 128), jnp.float32)
        for h in range(OWN_ROWS):
            picked = lane_take(pos_ref[r * OWN_ROWS + h : r * OWN_ROWS + h + 1, :], low)
            acc = jnp.where(high == h, picked, acc)
        for n in range(NPAIR):
            pay_ref[n, r : r + 1, :] = acc[n : n + 1, :]


def tet_gradient(corner):
    edge = [[corner[m + 1][r] - corner[0][r] for r in range(3)] for m in range(3)]
    total = [edge[0][r] + edge[1][r] + edge[2][r] for r in range(3)]
    squares = None
    for m in range(3):
        for r in range(3):
            term = edge[m][r] * edge[m][r]
            squares = term if squares is None else squares + term
    spread = total[0] * total[0] + total[1] * total[1] + total[2] * total[2]
    norm_sq = 2.0 * squares - 0.5 * spread

    def cross(a, b):
        return [
            a[1] * b[2] - a[2] * b[1],
            a[2] * b[0] - a[0] * b[2],
            a[0] * b[1] - a[1] * b[0],
        ]

    cof = [cross(edge[1], edge[2]), cross(edge[2], edge[0]), cross(edge[0], edge[1])]
    root2 = math.sqrt(2.0)
    det = root2 * (edge[0][0] * cof[0][0] + edge[0][1] * cof[0][1] + edge[0][2] * cof[0][2])
    root = jnp.sqrt(det * det + 4.0 * DELTA * DELTA)
    far = root + jnp.abs(det)
    height = jnp.where(det >= 0, 0.5 * far, (2.0 * DELTA * DELTA) / far)
    factor = (2.0 / 3.0) * jnp.exp((-2.0 / 3.0) * jnp.log(height))
    pull = (root2 / 3.0) * norm_sq / root
    grads = []
    for m in range(3):
        grads.append([factor * (2.0 * edge[m][r] - 0.5 * total[r] - pull * cof[m][r]) for r in range(3)])
    first = [-(grads[0][r] + grads[1][r] + grads[2][r]) for r in range(3)]
    return [first] + grads


def prepare_blocks(nodes_ref, packed_ref):
    turned = nodes_ref[...].T
    packed_ref[...] = jnp.concatenate([turned[0:64, :], turned[64:128, :]], axis=1)


def mark(chosen):
    return jnp.where(chosen, 1.0, 0.0).astype(jnp.bfloat16)


def build_marks(packed_ref, corners_ref, cols_ref, marks_ref, lanes_ref, slots_ref):
    node_iota = lax.broadcasted_iota(jnp.int32, (64, 128), 0)
    lane_iota = lax.broadcasted_iota(jnp.int32, (128, 128), 0)

    def corner_marks(g, carry):
        for i in range(4):
            block = g * 4 + i
            for c in range(4):
                ids = corners_ref[pl.ds(block * 4 + c, 1), :]
                marks_ref[block, :, c * 128 : (c + 1) * 128] = mark(node_iota == ids)
        return carry

    lax.fori_loop(0, 32, corner_marks, 0)

    def lane_marks(j, carry):
        low = packed_ref[pl.ds(pl.multiple_of(j * 8, 8), 8), :] & 127
        for i in range(8):
            lanes_ref[j, :, i * 128 : (i + 1) * 128] = mark(lane_iota == low[i : i + 1, :])
        return carry

    lax.fori_loop(0, 8, lane_marks, 0)
    for n in range(NPAIR):
        slots_ref[:, n * 128 : (n + 1) * 128] = mark(lane_iota == (cols_ref[n : n + 1, :] & 127))


def gather_own(pos_ref, packed_ref, part_ref):
    def body(g, carry):
        for i in range(2):
            rows = pl.ds(pl.multiple_of(g * 16 + i * 8, 8), 8)
            cols = packed_ref[rows, :]
            high = cols >> 7
            low = cols & 127
            for r in range(3):
                picked = jnp.zeros((8, 128), jnp.float32)
                for h in range(OWN_ROWS):
                    row = pos_ref[r * OWN_ROWS + h : r * OWN_ROWS + h + 1, :]
                    picked = jnp.where(high == h, lane_take(row, low), picked)
                part_ref[r, rows, :] = picked
        return carry

    lax.fori_loop(0, GROUPS, body, 0)


def tet_spread(j, ghost_ref, packed_ref, part_ref, corners_ref, spread_ref):
    base = pl.multiple_of(j * 8, 8)
    cols = packed_ref[pl.ds(base, 8), :]
    high = cols >> 7
    low = cols & 127
    source = []
    for r in range(3):
        picked = part_ref[r, pl.ds(base, 8), :]
        for n in range(NPAIR):
            picked = jnp.where(high == OWN_ROWS + n, lane_take(ghost_ref[n, r : r + 1, :], low), picked)
        source.append(picked)
    for half in range(2):
        block = half * 64 + base
        corner = []
        for c in range(4):
            lanes = corners_ref[pl.ds(block * 4 + c, 8, stride=4), :] + 64 * half
            corner.append([jnp.take_along_axis(source[r], lanes, axis=1, mode="promise_in_bounds") for r in range(3)])
        grads = tet_gradient(corner)
        for c in range(4):
            for r in range(3):
                start = (c * 6 + r) * 16 + half * 8
                spread_ref[start : start + 8, :] = grads[c][r]
                spread_ref[start + 48 : start + 56, :] = low_piece(grads[c][r])


def block_sums(j, spread_ref, marks_ref, pairs_ref):
    found = []
    for i in range(8):
        sums = []
        for half in range(2):
            rows = [
                spread_ref[pl.ds(c * 96 + half * 8 + i, 8, stride=16), :].astype(jnp.bfloat16) for c in range(4)
            ]
            sums.append(nt_dot(jnp.concatenate(rows, axis=1), marks_ref[half * 64 + j * 8 + i]))
        both = jnp.concatenate(sums, axis=1)
        pair = both[0:3, :] + both[3:6, :]
        pairs_ref[j * 8 + i, 0:3, :] = pair
        found.append(pair)
    return found


def row_group(j, pairs, packed_ref, lanes_ref, first, count):
    row_iota = lax.broadcasted_iota(jnp.int32, (count, 128), 0) + first
    high = packed_ref[pl.ds(pl.multiple_of(j * 8, 8), 8), :] >> 7
    left = []
    for i in range(8):
        pair = pairs[i]
        rest = low_piece(pair)
        chosen = row_iota == high[i : i + 1, :]
        stack = [jnp.where(chosen, pair[r : r + 1, :], 0.0) for r in range(3)]
        stack += [jnp.where(chosen, rest[r : r + 1, :], 0.0) for r in range(3)]
        left.append(jnp.concatenate(stack, axis=0).astype(jnp.bfloat16))
    return nt_dot(jnp.concatenate(left, axis=1), lanes_ref[j])


def ghost_rows(ghost_ref, packed_ref, part_ref, corners_ref, spreads, marks_ref, lanes_ref, pairs_ref, acc_ref):
    even_ref, odd_ref = spreads
    tets = functools.partial(tet_spread, ghost_ref=ghost_ref, packed_ref=packed_ref, part_ref=part_ref)

    def body(g, carry):
        pairs = block_sums(2 * g, even_ref, marks_ref, pairs_ref)
        tets(2 * g + 1, corners_ref=corners_ref, spread_ref=odd_ref)
        first = row_group(2 * g, pairs, packed_ref, lanes_ref, OWN_ROWS, GPAD)
        pairs = block_sums(2 * g + 1, odd_ref, marks_ref, pairs_ref)
        tets(jnp.minimum(2 * g + 2, 7), corners_ref=corners_ref, spread_ref=even_ref)
        second = row_group(2 * g + 1, pairs, packed_ref, lanes_ref, OWN_ROWS, GPAD)
        acc_ref[...] += first + second
        return carry

    acc_ref[...] = jnp.zeros_like(acc_ref)
    tets(0, corners_ref=corners_ref, spread_ref=even_ref)
    lax.fori_loop(0, 4, body, 0)


def own_rows(packed_ref, pairs_ref, lanes_ref, acc_ref):
    def body(g, carry):
        parts = []
        for half in range(2):
            j = 2 * g + half
            pairs = [pairs_ref[j * 8 + i, 0:3, :] for i in range(8)]
            parts.append(row_group(j, pairs, packed_ref, lanes_ref, 0, OWN_ROWS))
        acc_ref[...] += parts[0] + parts[1]
        return carry

    acc_ref[...] = jnp.zeros_like(acc_ref)
    lax.fori_loop(0, 4, body, 0)


def put_ghost_gradient(acc_ref, out_ref):
    for r in range(3):
        both = acc_ref[r * GPAD : (r + 1) * GPAD, :] + acc_ref[(3 + r) * GPAD : (4 + r) * GPAD, :]
        for n in range(NPAIR):
            out_ref[n, r : r + 1, :] = both[n : n + 1, :]


def returned_gradient(back_ref, cols_ref, slots_ref):
    high_iota = lax.broadcasted_iota(jnp.int32, (OWN_ROWS, 128), 0)
    left_parts = []
    for n in range(NPAIR):
        cols = cols_ref[n : n + 1, :]
        chosen = high_iota == (cols >> 7)
        values = jnp.where(cols >= 0, back_ref[n, 0:3, :], 0.0)
        rest = low_piece(values)
        stack = [jnp.where(chosen, values[r : r + 1, :], 0.0) for r in range(3)]
        stack += [jnp.where(chosen, rest[r : r + 1, :], 0.0) for r in range(3)]
        left_parts.append(jnp.concatenate(stack, axis=0).astype(jnp.bfloat16))
    out = nt_dot(jnp.concatenate(left_parts, axis=1), slots_ref[...])
    return out[0:48, :] + out[48:96, :]


def load_positions(raw_ref, pos_ref):
    for r in range(3):
        for h in range(OWN_ROWS):
            pos_ref[r * OWN_ROWS + h : r * OWN_ROWS + h + 1, :] = raw_ref[r : r + 1, h * 128 : (h + 1) * 128]


def store_positions(value, raw_ref):
    for r in range(3):
        for h in range(OWN_ROWS):
            raw_ref[r : r + 1, h * 128 : (h + 1) * 128] = value[r * OWN_ROWS + h : r * OWN_ROWS + h + 1, :]


FAR_FIRST = (2, 1, 3, 0)


def partners(sign):
    dom = lax.axis_index("dom")
    sub = lax.axis_index("sub")
    doms = lax.axis_size("dom")
    found = []
    for turn in FAR_FIRST:
        for k in (0, 4, 1, 3, 2):
            if k == REACH and turn == 0:
                continue
            there = lax.rem(dom + sign * (k - REACH) + doms, doms)
            found.append((k, turn, there, lax.rem(sub + turn, SUBS)))
    return found


def exchange(found, src_ref, dst_ref, send_sem, recv_sem):
    sub = lax.axis_index("sub")
    copies = []
    for k, turn, there, t in found:
        copies.append(
            pltpu.make_async_remote_copy(
                src_ref=src_ref.at[k * SUBS + t],
                dst_ref=dst_ref.at[k * SUBS + sub],
                send_sem=send_sem.at[k * SUBS + turn],
                recv_sem=recv_sem.at[k * SUBS + turn],
                device_id=(there, t),
                device_id_type=MESH,
            )
        )
    for copy in copies:
        copy.start()
    dst_ref[REACH * SUBS + sub] = src_ref[REACH * SUBS + sub]
    return copies


def smooth_kernel(
    raw_hbm,
    mask_hbm,
    list_hbm,
    count_hbm,
    nodes_hbm,
    corners_hbm,
    done_ref,
    raw_ref,
    mask_ref,
    list_ref,
    count_ref,
    nodes_ref,
    corners_ref,
    pos_ref,
    cols_ref,
    packed_ref,
    pay_ref,
    ghost_ref,
    out_ref,
    back_ref,
    part_ref,
    even_ref,
    odd_ref,
    marks_ref,
    lanes_ref,
    slots_ref,
    pairs_ref,
    ghost_acc,
    own_acc,
    load_sem,
    send_sem,
    recv_sem,
):
    ahead = partners(1)
    behind = partners(-1)
    barrier = pltpu.get_barrier_semaphore()
    for _, _, there, t in ahead:
        pl.semaphore_signal(barrier, inc=1, device_id=(there, t), device_id_type=MESH)
    sources = (raw_hbm, list_hbm, count_hbm, nodes_hbm, mask_hbm, corners_hbm)
    targets = (raw_ref, list_ref, count_ref, nodes_ref, mask_ref, corners_ref)
    loads = [pltpu.make_async_copy(sources[i], targets[i], load_sem.at[i]) for i in range(6)]
    for load in loads:
        load.start()
    for step in range(ITERS):
        for n in range(NPAIR):
            pay_ref[step, n, 3:4, :] = jnp.zeros((1, 128), jnp.float32)
            out_ref[step, n, 3:4, :] = jnp.zeros((1, 128), jnp.float32)
    for spread_ref in (even_ref, odd_ref):
        spread_ref[24 * 16 : 26 * 16, :] = jnp.zeros((32, 128), jnp.float32)
    for load in loads[0:3]:
        load.wait()
    load_positions(raw_ref, pos_ref)
    send_columns(list_ref, count_ref, cols_ref)
    gather_payload(pos_ref, cols_ref, pay_ref.at[0])
    for load in loads[3:6]:
        load.wait()
    pl.semaphore_wait(barrier, len(ahead))
    started = []
    for step in range(ITERS):
        copies = exchange(ahead, pay_ref.at[step], ghost_ref.at[step], send_sem.at[2 * step], recv_sem.at[2 * step])
        started += copies
        if step == 0:
            prepare_blocks(nodes_ref, packed_ref)
            build_marks(packed_ref, corners_ref, cols_ref, marks_ref, lanes_ref, slots_ref)
        gather_own(pos_ref, packed_ref, part_ref)
        for copy in copies:
            copy.wait_recv()
        ghost_rows(
            ghost_ref.at[step],
            packed_ref,
            part_ref,
            corners_ref,
            (even_ref, odd_ref),
            marks_ref,
            lanes_ref,
            pairs_ref,
            ghost_acc,
        )
        put_ghost_gradient(ghost_acc, out_ref.at[step])
        copies = exchange(
            behind, out_ref.at[step], back_ref.at[step], send_sem.at[2 * step + 1], recv_sem.at[2 * step + 1]
        )
        started += copies
        own_rows(packed_ref, pairs_ref, lanes_ref, own_acc)
        own = own_acc[0:48, :] + own_acc[48:96, :]
        free = jnp.where(mask_ref[...] == 0, STEP, 0.0)
        for copy in copies:
            copy.wait_recv()
        grad = own + returned_gradient(back_ref.at[step], cols_ref, slots_ref)
        value = pos_ref[...] - jnp.concatenate([free, free, free], axis=0) * grad
        if step < ITERS - 1:
            pos_ref[...] = value
            gather_payload(pos_ref, cols_ref, pay_ref.at[step + 1])
        else:
            store_positions(value, done_ref)
    for copy in started:
        copy.wait_send()


ANY = pl.BlockSpec(memory_space=pl.ANY)
VMEM = pl.BlockSpec(memory_space=pltpu.VMEM)


def per_device(positions, fixed_mask, send_count, send_list, block_nodes, tet_corners):
    corners = tet_corners.reshape(4, 128, 128).transpose(1, 0, 2).reshape(512, 128)
    mask = fixed_mask.reshape(OWN_ROWS, 128)
    counts = send_count.transpose(0, 1, 3, 2)
    inputs = (positions, mask, send_list, counts, block_nodes, corners)
    slots = pltpu.VMEM((ITERS, NPAIR, 4, 128), jnp.float32)
    return pl.pallas_call(
        smooth_kernel,
        out_shape=jax.ShapeDtypeStruct((3, 2048), jnp.float32),
        in_specs=[ANY] * 6,
        out_specs=VMEM,
        scratch_shapes=[pltpu.VMEM(x.shape, x.dtype) for x in inputs]
        + [
            pltpu.VMEM((48, 128), jnp.float32),
            pltpu.VMEM((NPAIR, 128), jnp.int32),
            pltpu.VMEM((64, 128), jnp.int32),
            slots,
            slots,
            slots,
            slots,
            pltpu.VMEM((3, 64, 128), jnp.float32),
            pltpu.VMEM((26 * 16, 128), jnp.float32),
            pltpu.VMEM((26 * 16, 128), jnp.float32),
            pltpu.VMEM((128, 64, 512), jnp.bfloat16),
            pltpu.VMEM((8, 128, 1024), jnp.bfloat16),
            pltpu.VMEM((128, NPAIR * 128), jnp.bfloat16),
            pltpu.VMEM((64, 8, 128), jnp.float32),
            pltpu.VMEM((6 * GPAD, 128), jnp.float32),
            pltpu.VMEM((6 * OWN_ROWS, 128), jnp.float32),
            pltpu.SemaphoreType.DMA((6,)),
            pltpu.SemaphoreType.DMA((2 * ITERS, NPAIR)),
            pltpu.SemaphoreType.DMA((2 * ITERS, NPAIR)),
        ],
        compiler_params=pltpu.CompilerParams(collective_id=0, has_side_effects=True),
        name="smooth",
    )(*inputs)


def solution(mesh):
    return jax.shard_map(
        per_device,
        mesh=mesh,
        in_specs=(
            P(None, ("dom", "sub")),
            P(("dom", "sub")),
            P("dom", "sub", None, None),
            P("dom", "sub", None, None, None),
            P(None, ("dom", "sub")),
            P(None, ("dom", "sub")),
        ),
        out_specs=P(None, ("dom", "sub")),
        check_vma=False,
    )
```

```python
import functools
import math

import jax
import jax.numpy as jnp
from jax import lax
from jax.experimental import pallas as pl
from jax.experimental.pallas import tpu as pltpu
from jax.sharding import PartitionSpec as P

ITERS = 2
STEP = 0.01
DELTA = 2.0
REACH = 2
SLOTS = 5
SUBS = 4
NPAIR = SLOTS * SUBS
OWN_ROWS = 16
ROWS = OWN_ROWS + NPAIR
GPAD = 24
GROUPS = 4
MESH = pl.DeviceIdType.MESH


def nt_dot(a, b):
    return lax.dot_general(a, b, (((1,), (1,)), ((), ())), preferred_element_type=jnp.float32)


def low_piece(x):
    return x - x.astype(jnp.bfloat16).astype(jnp.float32)


def lane_take(row, lanes):
    src = jnp.broadcast_to(row, lanes.shape)
    return jnp.take_along_axis(src, lanes, axis=1, mode="promise_in_bounds")


def send_columns(list_ref, count_ref, cols_ref):
    lane = lax.broadcasted_iota(jnp.int32, (1, 128), 1)
    for k in range(SLOTS):
        for t in range(SUBS):
            count = jnp.broadcast_to(count_ref[0, 0, t : t + 1, k : k + 1], (1, 128))
            row = list_ref[0, 0, k, t : t + 1, :]
            cols_ref[k * SUBS + t : k * SUBS + t + 1, :] = jnp.where(lane < count, row, -1)


def gather_payload(pos_ref, cols_ref, pay_ref):
    cols = jnp.concatenate([cols_ref[...], jnp.full((24 - NPAIR, 128), -1, jnp.int32)], axis=0)
    high = cols >> 7
    low = cols & 127
    for r in range(3):
        acc = jnp.zeros((24, 128), jnp.float32)
        for h in range(OWN_ROWS):
            picked = lane_take(pos_ref[r * OWN_ROWS + h : r * OWN_ROWS + h + 1, :], low)
            acc = jnp.where(high == h, picked, acc)
        for n in range(NPAIR):
            pay_ref[n, r : r + 1, :] = acc[n : n + 1, :]


def tet_gradient(corner):
    edge = [[corner[m + 1][r] - corner[0][r] for r in range(3)] for m in range(3)]
    total = [edge[0][r] + edge[1][r] + edge[2][r] for r in range(3)]
    squares = None
    for m in range(3):
        for r in range(3):
            term = edge[m][r] * edge[m][r]
            squares = term if squares is None else squares + term
    spread = total[0] * total[0] + total[1] * total[1] + total[2] * total[2]
    norm_sq = 2.0 * squares - 0.5 * spread

    def cross(a, b):
        return [
            a[1] * b[2] - a[2] * b[1],
            a[2] * b[0] - a[0] * b[2],
            a[0] * b[1] - a[1] * b[0],
        ]

    cof = [cross(edge[1], edge[2]), cross(edge[2], edge[0]), cross(edge[0], edge[1])]
    root2 = math.sqrt(2.0)
    det = root2 * (edge[0][0] * cof[0][0] + edge[0][1] * cof[0][1] + edge[0][2] * cof[0][2])
    root = jnp.sqrt(det * det + 4.0 * DELTA * DELTA)
    far = root + jnp.abs(det)
    height = jnp.where(det >= 0, 0.5 * far, (2.0 * DELTA * DELTA) / far)
    factor = (2.0 / 3.0) * jnp.exp((-2.0 / 3.0) * jnp.log(height))
    pull = (root2 / 3.0) * norm_sq / root
    grads = []
    for m in range(3):
        grads.append([factor * (2.0 * edge[m][r] - 0.5 * total[r] - pull * cof[m][r]) for r in range(3)])
    first = [-(grads[0][r] + grads[1][r] + grads[2][r]) for r in range(3)]
    return [first] + grads


def prepare_blocks(nodes_ref, packed_ref):
    turned = nodes_ref[...].T
    packed_ref[...] = jnp.concatenate([turned[0:64, :], turned[64:128, :]], axis=1)


def mark(chosen):
    return jnp.where(chosen, 1.0, 0.0).astype(jnp.bfloat16)


def build_marks(packed_ref, corners_ref, cols_ref, marks_ref, lanes_ref, slots_ref):
    node_iota = lax.broadcasted_iota(jnp.int32, (32, 128), 0)
    lane_iota = lax.broadcasted_iota(jnp.int32, (128, 128), 0)

    def corner_marks(g, carry):
        for i in range(4):
            block = g * 4 + i
            for c in range(4):
                ids = corners_ref[pl.ds(block * 4 + c, 1), :] & 31
                marks_ref[block, :, c * 128 : (c + 1) * 128] = mark(node_iota == ids)
        return carry

    lax.fori_loop(0, 32, corner_marks, 0)

    def lane_marks(j, carry):
        low = packed_ref[pl.ds(pl.multiple_of(j * 8, 8), 8), :] & 127
        for i in range(8):
            lanes_ref[j, :, i * 128 : (i + 1) * 128] = mark(lane_iota == low[i : i + 1, :])
        return carry

    lax.fori_loop(0, 8, lane_marks, 0)
    for n in range(NPAIR):
        slots_ref[:, n * 128 : (n + 1) * 128] = mark(lane_iota == (cols_ref[n : n + 1, :] & 127))


def gather_own(pos_ref, packed_ref, part_ref):
    def body(g, carry):
        for i in range(2):
            rows = pl.ds(pl.multiple_of(g * 16 + i * 8, 8), 8)
            cols = packed_ref[rows, :]
            high = cols >> 7
            low = cols & 127
            for r in range(3):
                picked = jnp.zeros((8, 128), jnp.float32)
                for h in range(OWN_ROWS):
                    row = pos_ref[r * OWN_ROWS + h : r * OWN_ROWS + h + 1, :]
                    picked = jnp.where(high == h, lane_take(row, low), picked)
                part_ref[r, rows, :] = picked
        return carry

    lax.fori_loop(0, GROUPS, body, 0)


def tet_spread(j, ghost_ref, packed_ref, part_ref, corners_ref, spread_ref):
    base = pl.multiple_of(j * 8, 8)
    cols = packed_ref[pl.ds(base, 8), :]
    high = cols >> 7
    low = cols & 127
    source = []
    for r in range(3):
        picked = part_ref[r, pl.ds(base, 8), :]
        for n in range(NPAIR):
            picked = jnp.where(high == OWN_ROWS + n, lane_take(ghost_ref[n, r : r + 1, :], low), picked)
        source.append(picked)
    for half in range(2):
        block = half * 64 + base
        corner = []
        for c in range(4):
            lanes = corners_ref[pl.ds(block * 4 + c, 8, stride=4), :] + 64 * half
            corner.append([jnp.take_along_axis(source[r], lanes, axis=1, mode="promise_in_bounds") for r in range(3)])
        grads = tet_gradient(corner)
        for c in range(4):
            for r in range(3):
                start = (c * 6 + r) * 16 + half * 8
                spread_ref[start : start + 8, :] = grads[c][r]
                spread_ref[start + 48 : start + 56, :] = low_piece(grads[c][r])


def block_sums(j, spread_ref, corners_ref, marks_ref, pairs_ref):
    found = []
    for i in range(8):
        sums = []
        for half in range(2):
            block = half * 64 + j * 8 + i
            parts = []
            for c in range(4):
                rows = spread_ref[pl.ds(c * 96 + half * 8 + i, 8, stride=16), :]
                upper = jnp.broadcast_to(corners_ref[pl.ds(block * 4 + c, 1), :], (8, 128)) >= 32
                split = [jnp.where(upper, 0.0, rows), jnp.where(upper, rows, 0.0)]
                parts.append(jnp.concatenate(split, axis=0).astype(jnp.bfloat16))
            out = nt_dot(jnp.concatenate(parts, axis=1), marks_ref[block])
            sums += [out[0:8, :], out[8:16, :]]
        both = jnp.concatenate(sums, axis=1)
        pair = both[0:3, :] + both[3:6, :]
        pairs_ref[j * 8 + i, 0:3, :] = pair
        found.append(pair)
    return found


def row_group(j, pairs, packed_ref, lanes_ref, first, count):
    row_iota = lax.broadcasted_iota(jnp.int32, (count, 128), 0) + first
    high = packed_ref[pl.ds(pl.multiple_of(j * 8, 8), 8), :] >> 7
    left = []
    for i in range(8):
        pair = pairs[i]
        rest = low_piece(pair)
        chosen = row_iota == high[i : i + 1, :]
        stack = [jnp.where(chosen, pair[r : r + 1, :], 0.0) for r in range(3)]
        stack += [jnp.where(chosen, rest[r : r + 1, :], 0.0) for r in range(3)]
        left.append(jnp.concatenate(stack, axis=0).astype(jnp.bfloat16))
    return nt_dot(jnp.concatenate(left, axis=1), lanes_ref[j])


def ghost_rows(ghost_ref, packed_ref, part_ref, corners_ref, spreads, marks_ref, lanes_ref, pairs_ref, acc_ref):
    tets = functools.partial(tet_spread, ghost_ref=ghost_ref, packed_ref=packed_ref, part_ref=part_ref)

    acc_ref[...] = jnp.zeros_like(acc_ref)
    tets(0, corners_ref=corners_ref, spread_ref=spreads[0])
    before = None
    for j in range(8):
        pairs = block_sums(j, spreads[j % 2], corners_ref, marks_ref, pairs_ref)
        if j < 7:
            tets(j + 1, corners_ref=corners_ref, spread_ref=spreads[(j + 1) % 2])
        if j > 0:
            acc_ref[...] += row_group(j - 1, before, packed_ref, lanes_ref, OWN_ROWS, GPAD)
        before = pairs
    acc_ref[...] += row_group(7, before, packed_ref, lanes_ref, OWN_ROWS, GPAD)


def own_rows(packed_ref, pairs_ref, lanes_ref, acc_ref):
    def body(g, carry):
        parts = []
        for half in range(2):
            j = 2 * g + half
            pairs = [pairs_ref[j * 8 + i, 0:3, :] for i in range(8)]
            parts.append(row_group(j, pairs, packed_ref, lanes_ref, 0, OWN_ROWS))
        acc_ref[...] += parts[0] + parts[1]
        return carry

    acc_ref[...] = jnp.zeros_like(acc_ref)
    lax.fori_loop(0, 4, body, 0)


def put_ghost_gradient(acc_ref, out_ref):
    for r in range(3):
        both = acc_ref[r * GPAD : (r + 1) * GPAD, :] + acc_ref[(3 + r) * GPAD : (4 + r) * GPAD, :]
        for n in range(NPAIR):
            out_ref[n, r : r + 1, :] = both[n : n + 1, :]


def returned_gradient(back_ref, cols_ref, slots_ref):
    high_iota = lax.broadcasted_iota(jnp.int32, (OWN_ROWS, 128), 0)
    left_parts = []
    for n in range(NPAIR):
        cols = cols_ref[n : n + 1, :]
        chosen = high_iota == (cols >> 7)
        values = jnp.where(cols >= 0, back_ref[n, 0:3, :], 0.0)
        rest = low_piece(values)
        stack = [jnp.where(chosen, values[r : r + 1, :], 0.0) for r in range(3)]
        stack += [jnp.where(chosen, rest[r : r + 1, :], 0.0) for r in range(3)]
        left_parts.append(jnp.concatenate(stack, axis=0).astype(jnp.bfloat16))
    out = nt_dot(jnp.concatenate(left_parts, axis=1), slots_ref[...])
    return out[0:48, :] + out[48:96, :]


def load_positions(raw_ref, pos_ref):
    for r in range(3):
        for h in range(OWN_ROWS):
            pos_ref[r * OWN_ROWS + h : r * OWN_ROWS + h + 1, :] = raw_ref[r : r + 1, h * 128 : (h + 1) * 128]


def store_positions(value, raw_ref):
    for r in range(3):
        for h in range(OWN_ROWS):
            raw_ref[r : r + 1, h * 128 : (h + 1) * 128] = value[r * OWN_ROWS + h : r * OWN_ROWS + h + 1, :]


FAR_FIRST = (2, 1, 3, 0)


def partners(sign):
    dom = lax.axis_index("dom")
    sub = lax.axis_index("sub")
    doms = lax.axis_size("dom")
    found = []
    for turn in FAR_FIRST:
        for k in (0, 4, 1, 3, 2):
            if k == REACH and turn == 0:
                continue
            there = lax.rem(dom + sign * (k - REACH) + doms, doms)
            found.append((k, turn, there, lax.rem(sub + turn, SUBS)))
    return found


def exchange(found, src_ref, dst_ref, send_sem, recv_sem):
    sub = lax.axis_index("sub")
    copies = []
    for k, turn, there, t in found:
        copies.append(
            pltpu.make_async_remote_copy(
                src_ref=src_ref.at[k * SUBS + t],
                dst_ref=dst_ref.at[k * SUBS + sub],
                send_sem=send_sem.at[k * SUBS + turn],
                recv_sem=recv_sem.at[k * SUBS + turn],
                device_id=(there, t),
                device_id_type=MESH,
            )
        )
    for copy in copies:
        copy.start()
    dst_ref[REACH * SUBS + sub] = src_ref[REACH * SUBS + sub]
    return copies


def smooth_kernel(
    raw_hbm,
    mask_hbm,
    list_hbm,
    count_hbm,
    nodes_hbm,
    corners_hbm,
    done_ref,
    raw_ref,
    mask_ref,
    list_ref,
    count_ref,
    nodes_ref,
    corners_ref,
    pos_ref,
    cols_ref,
    packed_ref,
    pay_ref,
    ghost_ref,
    out_ref,
    back_ref,
    part_ref,
    even_ref,
    odd_ref,
    marks_ref,
    lanes_ref,
    slots_ref,
    pairs_ref,
    ghost_acc,
    own_acc,
    shift_ref,
    load_sem,
    send_sem,
    recv_sem,
):
    ahead = partners(1)
    behind = partners(-1)
    barrier = pltpu.get_barrier_semaphore()
    for _, _, there, t in ahead:
        pl.semaphore_signal(barrier, inc=1, device_id=(there, t), device_id_type=MESH)
    sources = (raw_hbm, list_hbm, count_hbm, nodes_hbm, mask_hbm, corners_hbm)
    targets = (raw_ref, list_ref, count_ref, nodes_ref, mask_ref, corners_ref)
    loads = [pltpu.make_async_copy(sources[i], targets[i], load_sem.at[i]) for i in range(6)]
    for load in loads:
        load.start()
    for step in range(ITERS):
        for n in range(NPAIR):
            pay_ref[step, n, 3:4, :] = jnp.zeros((1, 128), jnp.float32)
            out_ref[step, n, 3:4, :] = jnp.zeros((1, 128), jnp.float32)
    for spread_ref in (even_ref, odd_ref):
        spread_ref[24 * 16 : 26 * 16, :] = jnp.zeros((32, 128), jnp.float32)
    for load in loads[0:3]:
        load.wait()
    load_positions(raw_ref, pos_ref)
    send_columns(list_ref, count_ref, cols_ref)
    gather_payload(pos_ref, cols_ref, pay_ref.at[0])
    for load in loads[3:6]:
        load.wait()
    pl.semaphore_wait(barrier, len(ahead))
    started = []
    for step in range(ITERS):
        copies = exchange(ahead, pay_ref.at[step], ghost_ref.at[step], send_sem.at[2 * step], recv_sem.at[2 * step])
        started += copies
        if step == 0:
            prepare_blocks(nodes_ref, packed_ref)
            build_marks(packed_ref, corners_ref, cols_ref, marks_ref, lanes_ref, slots_ref)
        gather_own(pos_ref, packed_ref, part_ref)
        for copy in copies:
            copy.wait_recv()
        ghost_rows(
            ghost_ref.at[step],
            packed_ref,
            part_ref,
            corners_ref,
            (even_ref, odd_ref),
            marks_ref,
            lanes_ref,
            pairs_ref,
            ghost_acc,
        )
        put_ghost_gradient(ghost_acc, out_ref.at[step])
        copies = exchange(
            behind, out_ref.at[step], back_ref.at[step], send_sem.at[2 * step + 1], recv_sem.at[2 * step + 1]
        )
        started += copies
        own_rows(packed_ref, pairs_ref, lanes_ref, own_acc)
        own = own_acc[0:48, :] + own_acc[48:96, :]
        free = jnp.where(mask_ref[...] == 0, STEP, 0.0)
        for copy in copies:
            copy.wait_recv()
        grad = own + returned_gradient(back_ref.at[step], cols_ref, slots_ref)
        shift = jnp.concatenate([free, free, free], axis=0) * grad
        if step > 0:
            total = shift_ref[...] + shift
        else:
            total = shift
        if step < ITERS - 1:
            shift_ref[...] = total
            pos_ref[...] = pos_ref[...] - shift
            gather_payload(pos_ref, cols_ref, pay_ref.at[step + 1])
        else:
            store_positions(total, done_ref)
    for copy in started:
        copy.wait_send()


ANY = pl.BlockSpec(memory_space=pl.ANY)
VMEM = pl.BlockSpec(memory_space=pltpu.VMEM)


def per_device(positions, fixed_mask, send_count, send_list, block_nodes, tet_corners):
    corners = tet_corners.reshape(4, 128, 128).transpose(1, 0, 2).reshape(512, 128)
    mask = fixed_mask.reshape(OWN_ROWS, 128)
    counts = send_count.transpose(0, 1, 3, 2)
    inputs = (positions, mask, send_list, counts, block_nodes, corners)
    slots = pltpu.VMEM((ITERS, NPAIR, 4, 128), jnp.float32)
    moved = pl.pallas_call(
        smooth_kernel,
        out_shape=jax.ShapeDtypeStruct((3, 2048), jnp.float32),
        in_specs=[ANY] * 6,
        out_specs=VMEM,
        scratch_shapes=[pltpu.VMEM(x.shape, x.dtype) for x in inputs]
        + [
            pltpu.VMEM((48, 128), jnp.float32),
            pltpu.VMEM((NPAIR, 128), jnp.int32),
            pltpu.VMEM((64, 128), jnp.int32),
            slots,
            slots,
            slots,
            slots,
            pltpu.VMEM((3, 64, 128), jnp.float32),
            pltpu.VMEM((26 * 16, 128), jnp.float32),
            pltpu.VMEM((26 * 16, 128), jnp.float32),
            pltpu.VMEM((128, 32, 512), jnp.bfloat16),
            pltpu.VMEM((8, 128, 1024), jnp.bfloat16),
            pltpu.VMEM((128, NPAIR * 128), jnp.bfloat16),
            pltpu.VMEM((64, 8, 128), jnp.float32),
            pltpu.VMEM((6 * GPAD, 128), jnp.float32),
            pltpu.VMEM((6 * OWN_ROWS, 128), jnp.float32),
            pltpu.VMEM((48, 128), jnp.float32),
            pltpu.SemaphoreType.DMA((6,)),
            pltpu.SemaphoreType.DMA((2 * ITERS, NPAIR)),
            pltpu.SemaphoreType.DMA((2 * ITERS, NPAIR)),
        ],
        compiler_params=pltpu.CompilerParams(collective_id=0, has_side_effects=True),
        name="smooth",
    )(*inputs)
    return positions - moved


def solution(mesh):
    return jax.shard_map(
        per_device,
        mesh=mesh,
        in_specs=(
            P(None, ("dom", "sub")),
            P(("dom", "sub")),
            P("dom", "sub", None, None),
            P("dom", "sub", None, None, None),
            P(None, ("dom", "sub")),
            P(None, ("dom", "sub")),
        ),
        out_specs=P(None, ("dom", "sub")),
        check_vma=False,
    )
```

```python
import functools
import math

import jax
import jax.numpy as jnp
from jax import lax
from jax.experimental import pallas as pl
from jax.experimental.pallas import tpu as pltpu
from jax.sharding import PartitionSpec as P

ITERS = 2
STEP = 0.01
DELTA = 2.0
REACH = 2
SLOTS = 5
SUBS = 4
NPAIR = SLOTS * SUBS
OWN_ROWS = 16
ROWS = OWN_ROWS + NPAIR
GPAD = 24
GROUPS = 4
MESH = pl.DeviceIdType.MESH


def nt_dot(a, b):
    return lax.dot_general(a, b, (((1,), (1,)), ((), ())), preferred_element_type=jnp.float32)


def low_piece(x):
    return x - x.astype(jnp.bfloat16).astype(jnp.float32)


def lane_take(row, lanes):
    src = jnp.broadcast_to(row, lanes.shape)
    return jnp.take_along_axis(src, lanes, axis=1, mode="promise_in_bounds")


def send_columns(list_ref, count_ref, cols_ref):
    lane = lax.broadcasted_iota(jnp.int32, (1, 128), 1)
    for k in range(SLOTS):
        for t in range(SUBS):
            count = jnp.broadcast_to(count_ref[0, 0, t : t + 1, k : k + 1], (1, 128))
            row = list_ref[0, 0, k, t : t + 1, :]
            cols_ref[k * SUBS + t : k * SUBS + t + 1, :] = jnp.where(lane < count, row, -1)


def gather_payload(pos_ref, cols_ref, pay_ref):
    cols = jnp.concatenate([cols_ref[...], jnp.full((24 - NPAIR, 128), -1, jnp.int32)], axis=0)
    high = cols >> 7
    low = cols & 127
    for r in range(3):
        acc = jnp.zeros((24, 128), jnp.float32)
        for h in range(OWN_ROWS):
            picked = lane_take(pos_ref[r * OWN_ROWS + h : r * OWN_ROWS + h + 1, :], low)
            acc = jnp.where(high == h, picked, acc)
        for n in range(NPAIR):
            pay_ref[n, r : r + 1, :] = acc[n : n + 1, :]


def tet_gradient(corner):
    edge = [[corner[m + 1][r] - corner[0][r] for r in range(3)] for m in range(3)]
    total = [edge[0][r] + edge[1][r] + edge[2][r] for r in range(3)]
    squares = None
    for m in range(3):
        for r in range(3):
            term = edge[m][r] * edge[m][r]
            squares = term if squares is None else squares + term
    spread = total[0] * total[0] + total[1] * total[1] + total[2] * total[2]
    norm_sq = 2.0 * squares - 0.5 * spread

    def cross(a, b):
        return [
            a[1] * b[2] - a[2] * b[1],
            a[2] * b[0] - a[0] * b[2],
            a[0] * b[1] - a[1] * b[0],
        ]

    cof = [cross(edge[1], edge[2]), cross(edge[2], edge[0]), cross(edge[0], edge[1])]
    root2 = math.sqrt(2.0)
    det = root2 * (edge[0][0] * cof[0][0] + edge[0][1] * cof[0][1] + edge[0][2] * cof[0][2])
    root = jnp.sqrt(det * det + 4.0 * DELTA * DELTA)
    far = root + jnp.abs(det)
    height = jnp.where(det >= 0, 0.5 * far, (2.0 * DELTA * DELTA) / far)
    factor = (2.0 / 3.0) * jnp.exp((-2.0 / 3.0) * jnp.log(height))
    pull = (root2 / 3.0) * norm_sq / root
    grads = []
    for m in range(3):
        grads.append([factor * (2.0 * edge[m][r] - 0.5 * total[r] - pull * cof[m][r]) for r in range(3)])
    first = [-(grads[0][r] + grads[1][r] + grads[2][r]) for r in range(3)]
    return [first] + grads


def prepare_blocks(nodes_ref, packed_ref):
    turned = nodes_ref[...].T
    packed_ref[...] = jnp.concatenate([turned[0:64, :], turned[64:128, :]], axis=1)


def mark(chosen):
    return jnp.where(chosen, 1.0, 0.0).astype(jnp.bfloat16)


def build_marks(packed_ref, corners_ref, cols_ref, marks_ref, lanes_ref, slots_ref):
    node_iota = lax.broadcasted_iota(jnp.int32, (32, 128), 0)
    lane_iota = lax.broadcasted_iota(jnp.int32, (128, 128), 0)

    def corner_marks(g, carry):
        for i in range(4):
            block = g * 4 + i
            for c in range(4):
                ids = corners_ref[pl.ds(block * 4 + c, 1), :] & 31
                marks_ref[block, :, c * 128 : (c + 1) * 128] = mark(node_iota == ids)
        return carry

    lax.fori_loop(0, 32, corner_marks, 0)

    def lane_marks(j, carry):
        low = packed_ref[pl.ds(pl.multiple_of(j * 8, 8), 8), :] & 127
        for i in range(8):
            lanes_ref[j, :, i * 128 : (i + 1) * 128] = mark(lane_iota == low[i : i + 1, :])
        return carry

    lax.fori_loop(0, 8, lane_marks, 0)
    for n in range(NPAIR):
        slots_ref[n] = mark(lane_iota == (cols_ref[n : n + 1, :] & 127))


def gather_own(pos_ref, packed_ref, part_ref):
    def body(g, carry):
        for i in range(2):
            rows = pl.ds(pl.multiple_of(g * 16 + i * 8, 8), 8)
            cols = packed_ref[rows, :]
            high = cols >> 7
            low = cols & 127
            for r in range(3):
                picked = jnp.zeros((8, 128), jnp.float32)
                for h in range(OWN_ROWS):
                    row = pos_ref[r * OWN_ROWS + h : r * OWN_ROWS + h + 1, :]
                    picked = jnp.where(high == h, lane_take(row, low), picked)
                part_ref[r, rows, :] = picked
        return carry

    lax.fori_loop(0, GROUPS, body, 0)


def gather_near(ghost_ref, packed_ref, part_ref, taken):
    def body(g, carry):
        for i in range(2):
            rows = pl.ds(pl.multiple_of(g * 16 + i * 8, 8), 8)
            cols = packed_ref[rows, :]
            high = cols >> 7
            low = cols & 127
            for r in range(3):
                picked = part_ref[r, rows, :]
                for n in taken:
                    picked = jnp.where(high == OWN_ROWS + n, lane_take(ghost_ref[n, r : r + 1, :], low), picked)
                part_ref[r, rows, :] = picked
        return carry

    lax.fori_loop(0, GROUPS, body, 0)


def tet_spread(j, taken, ghost_ref, packed_ref, part_ref, corners_ref, spread_ref):
    base = pl.multiple_of(j * 8, 8)
    cols = packed_ref[pl.ds(base, 8), :]
    high = cols >> 7
    low = cols & 127
    source = []
    for r in range(3):
        picked = part_ref[r, pl.ds(base, 8), :]
        for n in taken:
            picked = jnp.where(high == OWN_ROWS + n, lane_take(ghost_ref[n, r : r + 1, :], low), picked)
        source.append(picked)
    for half in range(2):
        block = half * 64 + base
        corner = []
        for c in range(4):
            lanes = corners_ref[pl.ds(block * 4 + c, 8, stride=4), :] + 64 * half
            corner.append([jnp.take_along_axis(source[r], lanes, axis=1, mode="promise_in_bounds") for r in range(3)])
        grads = tet_gradient(corner)
        for c in range(4):
            for r in range(3):
                start = (c * 6 + r) * 16 + half * 8
                spread_ref[start : start + 8, :] = grads[c][r]
                spread_ref[start + 48 : start + 56, :] = low_piece(grads[c][r])


def block_sums(j, spread_ref, corners_ref, marks_ref, pairs_ref):
    found = []
    for i in range(8):
        sums = []
        for half in range(2):
            block = half * 64 + j * 8 + i
            parts = []
            for c in range(4):
                rows = spread_ref[pl.ds(c * 96 + half * 8 + i, 8, stride=16), :]
                upper = jnp.broadcast_to(corners_ref[pl.ds(block * 4 + c, 1), :], (8, 128)) >= 32
                split = [jnp.where(upper, 0.0, rows), jnp.where(upper, rows, 0.0)]
                parts.append(jnp.concatenate(split, axis=0).astype(jnp.bfloat16))
            out = nt_dot(jnp.concatenate(parts, axis=1), marks_ref[block])
            sums += [out[0:8, :], out[8:16, :]]
        both = jnp.concatenate(sums, axis=1)
        pair = both[0:3, :] + both[3:6, :]
        pairs_ref[j * 8 + i, 0:3, :] = pair
        found.append(pair)
    return found


def row_group(j, pairs, packed_ref, lanes_ref, first, count):
    row_iota = lax.broadcasted_iota(jnp.int32, (count, 128), 0) + first
    high = packed_ref[pl.ds(pl.multiple_of(j * 8, 8), 8), :] >> 7
    left = []
    for i in range(8):
        pair = pairs[i]
        rest = low_piece(pair)
        chosen = row_iota == high[i : i + 1, :]
        stack = [jnp.where(chosen, pair[r : r + 1, :], 0.0) for r in range(3)]
        stack += [jnp.where(chosen, rest[r : r + 1, :], 0.0) for r in range(3)]
        left.append(jnp.concatenate(stack, axis=0).astype(jnp.bfloat16))
    return nt_dot(jnp.concatenate(left, axis=1), lanes_ref[j])


def ghost_rows(taken, ghost_ref, packed_ref, part_ref, corners_ref, spreads, marks_ref, lanes_ref, pairs_ref, acc_ref):
    tets = functools.partial(tet_spread, taken=taken, ghost_ref=ghost_ref, packed_ref=packed_ref, part_ref=part_ref)

    acc_ref[...] = jnp.zeros_like(acc_ref)
    tets(0, corners_ref=corners_ref, spread_ref=spreads[0])
    before = None
    for j in range(8):
        pairs = block_sums(j, spreads[j % 2], corners_ref, marks_ref, pairs_ref)
        if j < 7:
            tets(j + 1, corners_ref=corners_ref, spread_ref=spreads[(j + 1) % 2])
        if j > 0:
            acc_ref[...] += row_group(j - 1, before, packed_ref, lanes_ref, OWN_ROWS, GPAD)
        before = pairs
    acc_ref[...] += row_group(7, before, packed_ref, lanes_ref, OWN_ROWS, GPAD)


def own_rows(packed_ref, pairs_ref, lanes_ref, acc_ref):
    def body(g, carry):
        parts = []
        for half in range(2):
            j = 2 * g + half
            pairs = [pairs_ref[j * 8 + i, 0:3, :] for i in range(8)]
            parts.append(row_group(j, pairs, packed_ref, lanes_ref, 0, OWN_ROWS))
        acc_ref[...] += parts[0] + parts[1]
        return carry

    acc_ref[...] = jnp.zeros_like(acc_ref)
    lax.fori_loop(0, 4, body, 0)


def put_ghost_gradient(acc_ref, out_ref):
    for r in range(3):
        both = acc_ref[r * GPAD : (r + 1) * GPAD, :] + acc_ref[(3 + r) * GPAD : (4 + r) * GPAD, :]
        for n in range(NPAIR):
            out_ref[n, r : r + 1, :] = both[n : n + 1, :]


def returned_gradient(back_ref, cols_ref, slots_ref, taken):
    high_iota = lax.broadcasted_iota(jnp.int32, (OWN_ROWS, 128), 0)
    left_parts = []
    right_parts = []
    for n in taken:
        cols = cols_ref[pl.ds(n, 1), :]
        chosen = high_iota == (cols >> 7)
        values = jnp.where(cols >= 0, back_ref[n, 0:3, :], 0.0)
        rest = low_piece(values)
        stack = [jnp.where(chosen, values[r : r + 1, :], 0.0) for r in range(3)]
        stack += [jnp.where(chosen, rest[r : r + 1, :], 0.0) for r in range(3)]
        left_parts.append(jnp.concatenate(stack, axis=0).astype(jnp.bfloat16))
        right_parts.append(slots_ref[n])
    out = nt_dot(jnp.concatenate(left_parts, axis=1), jnp.concatenate(right_parts, axis=1))
    return out[0:48, :] + out[48:96, :]


def load_positions(raw_ref, pos_ref):
    for r in range(3):
        for h in range(OWN_ROWS):
            pos_ref[r * OWN_ROWS + h : r * OWN_ROWS + h + 1, :] = raw_ref[r : r + 1, h * 128 : (h + 1) * 128]


def store_positions(value, raw_ref):
    for r in range(3):
        for h in range(OWN_ROWS):
            raw_ref[r : r + 1, h * 128 : (h + 1) * 128] = value[r * OWN_ROWS + h : r * OWN_ROWS + h + 1, :]


FAR_FIRST = (2, 1, 3, 0)


def partners(sign):
    dom = lax.axis_index("dom")
    sub = lax.axis_index("sub")
    doms = lax.axis_size("dom")
    found = []
    for turn in FAR_FIRST:
        for k in (0, 4, 1, 3, 2):
            if k == REACH and turn == 0:
                continue
            there = lax.rem(dom + sign * (k - REACH) + doms, doms)
            found.append((k, turn, there, lax.rem(sub + turn, SUBS)))
    return found


def exchange(found, src_ref, dst_ref, send_sem, recv_sem):
    sub = lax.axis_index("sub")
    copies = []
    for k, turn, there, t in found:
        copies.append(
            pltpu.make_async_remote_copy(
                src_ref=src_ref.at[k * SUBS + t],
                dst_ref=dst_ref.at[k * SUBS + sub],
                send_sem=send_sem.at[k * SUBS + turn],
                recv_sem=recv_sem.at[k * SUBS + turn],
                device_id=(there, t),
                device_id_type=MESH,
            )
        )
    for copy in copies:
        copy.start()
    dst_ref[REACH * SUBS + sub] = src_ref[REACH * SUBS + sub]
    return copies


def smooth_kernel(
    raw_hbm,
    mask_hbm,
    list_hbm,
    count_hbm,
    nodes_hbm,
    corners_hbm,
    done_ref,
    raw_ref,
    mask_ref,
    list_ref,
    count_ref,
    nodes_ref,
    corners_ref,
    pos_ref,
    cols_ref,
    packed_ref,
    pay_ref,
    ghost_ref,
    out_ref,
    back_ref,
    part_ref,
    even_ref,
    odd_ref,
    marks_ref,
    lanes_ref,
    slots_ref,
    pairs_ref,
    ghost_acc,
    own_acc,
    shift_ref,
    load_sem,
    send_sem,
    recv_sem,
):
    ahead = partners(1)
    behind = partners(-1)
    barrier = pltpu.get_barrier_semaphore()
    for _, _, there, t in ahead:
        pl.semaphore_signal(barrier, inc=1, device_id=(there, t), device_id_type=MESH)
    sources = (raw_hbm, list_hbm, count_hbm, nodes_hbm, mask_hbm, corners_hbm)
    targets = (raw_ref, list_ref, count_ref, nodes_ref, mask_ref, corners_ref)
    loads = [pltpu.make_async_copy(sources[i], targets[i], load_sem.at[i]) for i in range(6)]
    for load in loads:
        load.start()
    for step in range(ITERS):
        for n in range(NPAIR):
            pay_ref[step, n, 3:4, :] = jnp.zeros((1, 128), jnp.float32)
            out_ref[step, n, 3:4, :] = jnp.zeros((1, 128), jnp.float32)
    for spread_ref in (even_ref, odd_ref):
        spread_ref[24 * 16 : 26 * 16, :] = jnp.zeros((32, 128), jnp.float32)
    for load in loads[0:3]:
        load.wait()
    load_positions(raw_ref, pos_ref)
    send_columns(list_ref, count_ref, cols_ref)
    gather_payload(pos_ref, cols_ref, pay_ref.at[0])
    for load in loads[3:6]:
        load.wait()
    pl.semaphore_wait(barrier, len(ahead))
    sub = lax.axis_index("sub")
    far = [k * SUBS + lax.rem(sub + 2, SUBS) for k in range(SLOTS)]
    near = [k * SUBS + lax.rem(sub + turn, SUBS) for k in range(SLOTS) for turn in (0, 1, 3)]
    started = []
    for step in range(ITERS):
        copies = exchange(ahead, pay_ref.at[step], ghost_ref.at[step], send_sem.at[2 * step], recv_sem.at[2 * step])
        started += copies
        if step == 0:
            prepare_blocks(nodes_ref, packed_ref)
            build_marks(packed_ref, corners_ref, cols_ref, marks_ref, lanes_ref, slots_ref)
        gather_own(pos_ref, packed_ref, part_ref)
        for copy, partner in zip(copies, ahead):
            if partner[1] != 2:
                copy.wait_recv()
        gather_near(ghost_ref.at[step], packed_ref, part_ref, near)
        for copy, partner in zip(copies, ahead):
            if partner[1] == 2:
                copy.wait_recv()
        ghost_rows(
            far,
            ghost_ref.at[step],
            packed_ref,
            part_ref,
            corners_ref,
            (even_ref, odd_ref),
            marks_ref,
            lanes_ref,
            pairs_ref,
            ghost_acc,
        )
        put_ghost_gradient(ghost_acc, out_ref.at[step])
        copies = exchange(
            behind, out_ref.at[step], back_ref.at[step], send_sem.at[2 * step + 1], recv_sem.at[2 * step + 1]
        )
        started += copies
        own_rows(packed_ref, pairs_ref, lanes_ref, own_acc)
        own = own_acc[0:48, :] + own_acc[48:96, :]
        free = jnp.where(mask_ref[...] == 0, STEP, 0.0)
        for copy, partner in zip(copies, behind):
            if partner[1] != 2:
                copy.wait_recv()
        own = own + returned_gradient(back_ref.at[step], cols_ref, slots_ref, near)
        for copy, partner in zip(copies, behind):
            if partner[1] == 2:
                copy.wait_recv()
        grad = own + returned_gradient(back_ref.at[step], cols_ref, slots_ref, far)
        shift = jnp.concatenate([free, free, free], axis=0) * grad
        if step > 0:
            total = shift_ref[...] + shift
        else:
            total = shift
        if step < ITERS - 1:
            shift_ref[...] = total
            pos_ref[...] = pos_ref[...] - shift
            gather_payload(pos_ref, cols_ref, pay_ref.at[step + 1])
        else:
            store_positions(total, done_ref)
    for copy in started:
        copy.wait_send()


ANY = pl.BlockSpec(memory_space=pl.ANY)
VMEM = pl.BlockSpec(memory_space=pltpu.VMEM)


def per_device(positions, fixed_mask, send_count, send_list, block_nodes, tet_corners):
    corners = tet_corners.reshape(4, 128, 128).transpose(1, 0, 2).reshape(512, 128)
    mask = fixed_mask.reshape(OWN_ROWS, 128)
    counts = send_count.transpose(0, 1, 3, 2)
    inputs = (positions, mask, send_list, counts, block_nodes, corners)
    slots = pltpu.VMEM((ITERS, NPAIR, 4, 128), jnp.float32)
    moved = pl.pallas_call(
        smooth_kernel,
        out_shape=jax.ShapeDtypeStruct((3, 2048), jnp.float32),
        in_specs=[ANY] * 6,
        out_specs=VMEM,
        scratch_shapes=[pltpu.VMEM(x.shape, x.dtype) for x in inputs]
        + [
            pltpu.VMEM((48, 128), jnp.float32),
            pltpu.VMEM((NPAIR, 128), jnp.int32),
            pltpu.VMEM((64, 128), jnp.int32),
            slots,
            slots,
            slots,
            slots,
            pltpu.VMEM((3, 64, 128), jnp.float32),
            pltpu.VMEM((26 * 16, 128), jnp.float32),
            pltpu.VMEM((26 * 16, 128), jnp.float32),
            pltpu.VMEM((128, 32, 512), jnp.bfloat16),
            pltpu.VMEM((8, 128, 1024), jnp.bfloat16),
            pltpu.VMEM((NPAIR, 128, 128), jnp.bfloat16),
            pltpu.VMEM((64, 8, 128), jnp.float32),
            pltpu.VMEM((6 * GPAD, 128), jnp.float32),
            pltpu.VMEM((6 * OWN_ROWS, 128), jnp.float32),
            pltpu.VMEM((48, 128), jnp.float32),
            pltpu.SemaphoreType.DMA((6,)),
            pltpu.SemaphoreType.DMA((2 * ITERS, NPAIR)),
            pltpu.SemaphoreType.DMA((2 * ITERS, NPAIR)),
        ],
        compiler_params=pltpu.CompilerParams(collective_id=0, has_side_effects=True),
        name="smooth",
    )(*inputs)
    return positions - moved


def solution(mesh):
    return jax.shard_map(
        per_device,
        mesh=mesh,
        in_specs=(
            P(None, ("dom", "sub")),
            P(("dom", "sub")),
            P("dom", "sub", None, None),
            P("dom", "sub", None, None, None),
            P(None, ("dom", "sub")),
            P(None, ("dom", "sub")),
        ),
        out_specs=P(None, ("dom", "sub")),
        check_vma=False,
    )
```
